256 devices in a mesh: dp: 4 (over x), context: 32 (over y, z), head: 2 (over core).
Axes of the slice: x: 4, y: 4, z: 8, core: 2. Of those that a mesh axis runs over, the one named last changes fastest.
Arguments:
- tokens: bfloat16 [4, 2, 4096, 4096], P('dp', None, 'context', 'head'), may hold values from -7 to 7
- queries: bfloat16 [4, 2, 4096, 2048], P('dp', None, 'context', 'head'), may hold values from -160 to 160
- grad_out: bfloat16 [4, 2, 4096, 2048], P('dp', None, 'context', 'head'), may hold values from -6 to 6
- w_key: bfloat16 [4096, 256], P('context', 'head'), may hold values from -0.09375 to 0.09375
- w_value: bfloat16 [4096, 256], P('context', 'head'), may hold values from -0.09375 to 0.09375
- block_len: int32 [4], P('dp'), may hold values from 8 to 32, as said below
Outputs:
- grad_query: bfloat16 [4, 2, 4096, 2048], P('dp', None, 'context', 'head')
- grad_x: bfloat16 [4, 2, 4096, 4096], P('dp', None, 'context', 'head')
- grad_wkey: float32 [4096, 256], P('context', 'head')
- grad_wvalue: float32 [4096, 256], P('context', 'head')
The draws below stay inside these ranges and needn't reach their ends.
Inputs may be any that keep to these rules, and one draw needn't show every extreme that they name: `block_len`: each entry is 8, 16 or 32.
All inputs are finite; a program needn't handle non-finite values.
Results may differ from the reference program's by a relative error of at most 0.025.
Values may be sent and summed in bfloat16 or wider, within the bound.
No kernel may reach another device: no remote copies, remote signals or barrier semaphores. Data moves between devices by JAX's collectives and lax.ppermute only.
A program may use at most 64 MiB of HBM per device.

```python
import math
import jax
import jax.numpy as jnp
from jax import lax

D = 4096
HEADS = 16
KV_HEADS = 2
HEAD_DIM = 128
CL_DEV = 128
LC = 4096
REPLICAS = 4
N_CONTEXT = 32


def shared_arrays(key):
    token_key, weight_key, query_key = jax.random.split(jax.random.fold_in(key, 11), 3)
    length = CL_DEV * N_CONTEXT
    tokens = jnp.clip(jax.random.normal(token_key, (REPLICAS, 2, length, D), jnp.float32), -6.0, 6.0)
    w_key = jnp.clip(jax.random.normal(weight_key, (D, KV_HEADS * HEAD_DIM), jnp.float32), -6.0, 6.0) / math.sqrt(D)
    queries = jnp.clip(jax.random.normal(query_key, (REPLICAS, 2, length, HEADS * HEAD_DIM), jnp.float32), -6.0, 6.0)
    return (tokens, w_key, queries)


def draw_tokens(key, part):
    return shared_arrays(key)[0].astype(jnp.bfloat16)


def draw_w_key(key, part):
    return shared_arrays(key)[1].astype(jnp.bfloat16)


def draw_queries(key, part):
    return shared_arrays(key)[2].astype(jnp.bfloat16)


def draw_block_len(key, part):
    order = jax.random.permutation(jax.random.fold_in(key, 7), jnp.arange(REPLICAS, dtype=jnp.int32))
    exponent = 3 + order % 3
    return jnp.left_shift(jnp.ones((REPLICAS,), jnp.int32), exponent.astype(jnp.int32))


def level_of(own_key, dims, shards, low, top_value):
    loudness, own = 1.0, jax.random.fold_in(own_key, 6)
    for axis_at, parts in shards:
        draws = jnp.exp(jax.random.uniform(jax.random.fold_in(own, axis_at), (parts,), jnp.float32, low / len(shards), top_value / len(shards)))
        loudness = loudness * jnp.repeat(draws, dims[axis_at] // parts).reshape([-1 if axis == axis_at else 1 for axis in range(len(dims))])
    return loudness


def normal_values(key, dims, deviation, bound, cuts=(), kind=jnp.bfloat16):
    result = jax.random.normal(key, dims, jnp.float32) * deviation
    if len(cuts) > 0:
        result = level_of(key, dims, cuts, -0.22, 0.18) * result
    return jnp.clip(result, min=-bound, max=bound).astype(kind)


def setup_inputs(seed: int = 0) -> dict:
    arg_keys = jax.random.split(jax.random.key(seed), 7)
    tokens = draw_tokens(jax.random.fold_in(arg_keys[6], 71), 0)
    queries = draw_queries(jax.random.fold_in(arg_keys[6], 71), 0)
    grad_out = normal_values(arg_keys[2], (REPLICAS, 2, LC, HEADS * HEAD_DIM), 1.0, 6.0, ((0, 4), (2, 32), (3, 2)))
    w_key = draw_w_key(jax.random.fold_in(arg_keys[6], 71), 0)
    w_value = normal_values(arg_keys[4], (D, KV_HEADS * HEAD_DIM), D ** -0.5, 0.09375, ((0, 32), (1, 2)))
    block_len = draw_block_len(jax.random.fold_in(arg_keys[6], 71), 0)
    return {"tokens": tokens, "queries": queries, "grad_out": grad_out, "w_key": w_key, "w_value": w_value, "block_len": block_len}


masked_score = -1e+30

def rounded(values):
    return lax.optimization_barrier(values.astype(jnp.bfloat16)).astype(jnp.float32)

def matmul(left, right):
    return jnp.dot(left, right, precision=lax.Precision.HIGHEST)

def tile_einsum(form, left, right):
    return jnp.einsum(form, left, right, precision=lax.Precision.HIGHEST)

def one_head(q_clean, q_noisy, g_clean, g_noisy, k_clean, v_clean, k_noisy, v_noisy, block_size):
    score_scale = 1.0 / math.sqrt(HEAD_DIM)
    length = CL_DEV * N_CONTEXT
    position = jnp.arange(length, dtype=jnp.int32) // block_size
    see_clean = position[None, :] <= position[:, None]
    see_cross = position[None, :] < position[:, None]
    local_block = jnp.arange(CL_DEV, dtype=jnp.int32) // block_size
    see_own = local_block[None, :] == local_block[:, None]
    tile_shape = (N_CONTEXT, CL_DEV, HEAD_DIM)
    qn_tiles = q_noisy.reshape(tile_shape)
    gn_tiles = g_noisy.reshape(tile_shape)
    kn_tiles = k_noisy.reshape(tile_shape)
    vn_tiles = v_noisy.reshape(tile_shape)
    s_cc = jnp.where(see_clean, matmul(q_clean, k_clean.T) * score_scale, masked_score)
    s_nc = jnp.where(see_cross, matmul(q_noisy, k_clean.T) * score_scale, masked_score)
    s_nn = jnp.where(see_own, tile_einsum('tqd,tkd->tqk', qn_tiles, kn_tiles) * score_scale, masked_score)
    peak_c = lax.optimization_barrier(jnp.max(s_cc, axis=1))
    lse_c = peak_c + jnp.log(lax.optimization_barrier(jnp.sum(jnp.exp(s_cc - peak_c[:, None]), axis=1)))
    peak_n = jnp.maximum(lax.optimization_barrier(jnp.max(s_nc, axis=1)), lax.optimization_barrier(jnp.max(s_nn, axis=2)).reshape(length))
    peak_tiles = peak_n.reshape(N_CONTEXT, CL_DEV)
    total_n = lax.optimization_barrier(jnp.sum(jnp.exp(s_nc - peak_n[:, None]), axis=1))
    total_n = total_n + lax.optimization_barrier(jnp.sum(jnp.exp(s_nn - peak_tiles[:, :, None]), axis=2)).reshape(length)
    lse_n = peak_n + jnp.log(total_n)
    p_cc = jnp.exp(s_cc - lse_c[:, None])
    p_nc = jnp.exp(s_nc - lse_n[:, None])
    p_nn = jnp.exp(s_nn - lse_n.reshape(N_CONTEXT, CL_DEV)[:, :, None])
    half_cc = rounded(p_cc)
    half_nc = rounded(p_nc)
    half_nn = rounded(p_nn)
    out_c = matmul(half_cc, v_clean)
    out_n = matmul(half_nc, v_clean) + tile_einsum('tqk,tkd->tqd', half_nn, vn_tiles).reshape(length, HEAD_DIM)
    delta_c = lax.optimization_barrier(jnp.sum(g_clean * out_c, axis=1))
    delta_n = lax.optimization_barrier(jnp.sum(g_noisy * out_n, axis=1))
    ds_cc = rounded(p_cc * (matmul(g_clean, v_clean.T) - delta_c[:, None]))
    ds_nc = rounded(p_nc * (matmul(g_noisy, v_clean.T) - delta_n[:, None]))
    dp_nn = tile_einsum('tqd,tkd->tqk', gn_tiles, vn_tiles)
    ds_nn = rounded(p_nn * (dp_nn - delta_n.reshape(N_CONTEXT, CL_DEV)[:, :, None]))
    dq_c = matmul(ds_cc, k_clean) * score_scale
    dq_n = (matmul(ds_nc, k_clean) + tile_einsum('tqk,tkd->tqd', ds_nn, kn_tiles).reshape(length, HEAD_DIM)) * score_scale
    dk_c = (matmul(ds_cc.T, q_clean) + matmul(ds_nc.T, q_noisy)) * score_scale
    dv_c = matmul(half_cc.T, g_clean) + matmul(half_nc.T, g_noisy)
    dk_n = tile_einsum('tqk,tqd->tkd', ds_nn, qn_tiles).reshape(length, HEAD_DIM) * score_scale
    dv_n = tile_einsum('tqk,tqd->tkd', half_nn, gn_tiles).reshape(length, HEAD_DIM)
    return (jnp.stack([dq_c, dq_n]), jnp.stack([dk_c, dk_n]), jnp.stack([dv_c, dv_n]))

def reference(tokens, queries, grad_out, w_key, w_value, block_len):
    length = CL_DEV * N_CONTEXT
    group_size = HEADS // KV_HEADS
    flat_tokens = tokens.reshape(-1, D)
    key_flat = jnp.dot(flat_tokens, w_key, preferred_element_type=jnp.float32).astype(jnp.bfloat16)
    value_flat = jnp.dot(flat_tokens, w_value, preferred_element_type=jnp.float32).astype(jnp.bfloat16)

    def by_head(array, head_count):
        shaped = array.astype(jnp.float32).reshape(REPLICAS, 2, length, head_count, HEAD_DIM)
        return shaped.transpose(0, 3, 1, 2, 4).reshape(REPLICAS * head_count, 2, length, HEAD_DIM)
    key_heads = by_head(key_flat, KV_HEADS)
    value_heads = by_head(value_flat, KV_HEADS)
    query_heads = by_head(queries, HEADS)
    grad_heads = by_head(grad_out, HEADS)
    items = jnp.arange(REPLICAS * HEADS, dtype=jnp.int32)

    def run_item(index):
        replica = index // HEADS
        kv_index = replica * KV_HEADS + index % HEADS // group_size
        q_head = query_heads[index]
        g_head = grad_heads[index]
        k_head = key_heads[kv_index]
        v_head = value_heads[kv_index]
        return one_head(q_head[0], q_head[1], g_head[0], g_head[1], k_head[0], v_head[0], k_head[1], v_head[1], block_len[replica])
    dq_items, dk_items, dv_items = lax.map(run_item, items)
    grad_query = dq_items.reshape(REPLICAS, HEADS, 2, length, HEAD_DIM).transpose(0, 2, 3, 1, 4)
    grad_query = grad_query.reshape(REPLICAS, 2, length, HEADS * HEAD_DIM).astype(jnp.bfloat16)

    def group_sum(items_grad):
        summed = items_grad.reshape(REPLICAS, KV_HEADS, group_size, 2, length, HEAD_DIM).sum(axis=2)
        summed = summed.transpose(0, 2, 3, 1, 4).reshape(REPLICAS * 2 * length, KV_HEADS * HEAD_DIM)
        return summed.astype(jnp.bfloat16)
    grad_key = group_sum(dk_items)
    grad_value = group_sum(dv_items)
    grad_x = jnp.dot(grad_key, w_key.T, preferred_element_type=jnp.float32)
    grad_x = grad_x + jnp.dot(grad_value, w_value.T, preferred_element_type=jnp.float32)
    grad_x = grad_x.astype(jnp.bfloat16).reshape(tokens.shape)
    grad_wkey = jnp.dot(flat_tokens.T, grad_key, preferred_element_type=jnp.float32)
    grad_wvalue = jnp.dot(flat_tokens.T, grad_value, preferred_element_type=jnp.float32)
    return (grad_query, grad_x, grad_wkey, grad_wvalue)
```

```python
import math

import jax
import jax.numpy as jnp
from jax import lax
from jax.experimental import pallas as pl
from jax.experimental.pallas import tpu as pltpu
from jax.sharding import Mesh
from jax.sharding import PartitionSpec as P

HEAD_DIM = 128
CONTEXT = ("context_0", "context_1")
BF16 = jnp.bfloat16
F32 = jnp.float32
MASKED = -1e30
SCALE = 1.0 / math.sqrt(HEAD_DIM)
EXP_SCALE = math.log2(math.e) / math.sqrt(HEAD_DIM)
BLOCK = 256
CHUNKS = 4


def dot(left, right):
    return jnp.dot(left, right, preferred_element_type=F32)


def shifted(array, axis, step):
    size = lax.axis_size(axis)
    return lax.ppermute(array, axis, [(i, (i + step) % size) for i in range(size)])


def mirrored(array):
    size = lax.axis_size(CONTEXT)
    return lax.ppermute(array, CONTEXT, [(i, size - 1 - i) for i in range(size)])


def turned_over(array, axis):
    size = lax.axis_size(axis)
    return lax.ppermute(array, axis, [(i, size - 1 - i) for i in range(size)])


def swapped(array):
    return lax.ppermute(array, "head", [(0, 1), (1, 0)])


def gather_z(array):
    copies = jnp.broadcast_to(array, (lax.axis_size("context_1"), *array.shape))
    tiles = lax.all_to_all(copies, "context_1", 0, 0, tiled=True)
    return tiles.reshape(-1, *array.shape[1:])


def gather_ring(array, axis):
    half = array.shape[0] // 2
    before = shifted(array, axis, 1)
    after = shifted(array, axis, -1)
    far_low = shifted(before[:half], axis, 1)
    far_high = shifted(after[half:], axis, -1)
    return array, before, jnp.concatenate([far_low, far_high], axis=0), after


def reduce_ring(pieces, axis):
    own, before, far_low, far_high, after = pieces
    half = far_low.shape[0]
    got_low = shifted(far_low, axis, 1)
    got_high = shifted(far_high, axis, -1)
    up = jnp.concatenate(
        [(after[:half].astype(F32) + got_low.astype(F32)).astype(BF16), after[half:]], axis=0
    )
    down = jnp.concatenate(
        [before[:half], (before[half:].astype(F32) + got_high.astype(F32)).astype(BF16)], axis=0
    )
    from_before = shifted(up, axis, 1)
    from_after = shifted(down, axis, -1)
    return own.astype(F32) + from_before.astype(F32) + from_after.astype(F32)


def scatter_z(array):
    size = lax.axis_size("context_1")
    tiles = array.reshape(size, array.shape[0] // size, array.shape[1])
    tiles = lax.all_to_all(tiles, "context_1", 0, 0, tiled=True)
    return jnp.sum(tiles.astype(F32), axis=0)


def attention_kernel(
    info,
    q_clean,
    g_clean,
    q_noisy,
    g_noisy,
    kv_0,
    kv_1,
    kv_2,
    kv_3,
    kv_own,
    dq_clean,
    dq_noisy,
    out_0,
    out_1,
    out_2a,
    out_2b,
    out_3,
    out_own,
    kvs,
    qh,
    gh,
    qt,
    gt,
    weights,
    gprobs,
    weights_own,
    gprobs_own,
    peak,
    total,
    moment,
    used,
    used_own,
    dqt,
    acc,
):
    row_y = info[0]
    tile_clean = info[1]
    tile_noisy = info[2]
    shift = info[3]
    blocks_y = 4
    full_clean = tile_clean >> 1
    full_noisy = tile_noisy >> 1
    for part, source in enumerate((kv_0, kv_1, kv_2, kv_3)):
        place = ((row_y - part) & 3) * blocks_y
        for b in range(blocks_y):
            kvs[place + b] = source[b * BLOCK : (b + 1) * BLOCK, :]
    for stream, (q_ref, g_ref) in enumerate(((q_clean, g_clean), (q_noisy, g_noisy))):
        for h in range(2 * CHUNKS):
            at = slice((h % 2) * HEAD_DIM, (h % 2 + 1) * HEAD_DIM)
            for ref, rows, turned in ((q_ref, qh, qt), (g_ref, gh, gt)):
                tile = ref[:, h * HEAD_DIM : (h + 1) * HEAD_DIM]
                rows[stream, h // 2, at, :] = tile
                turned[stream, h // 2, :, at] = tile.T
    acc[...] = jnp.zeros_like(acc)

    lane = lax.broadcasted_iota(jnp.int32, (1, BLOCK), 1) & (HEAD_DIM - 1)

    def limits(tile, after):
        pos = tile * HEAD_DIM + lane
        return ((pos >> shift) + after) << shift

    def step_forward(stream, k, v, j, visible, first, save_w, save_g, save_used):
        s = dot(k, qt[stream, j])
        d = dot(v, gt[stream, j])
        if visible is not None:
            s = jnp.where(visible, s, MASKED)
        top = jnp.max(s, axis=0, keepdims=True)
        if first:
            new_peak = top
        else:
            old_peak = peak[stream, j]
            new_peak = jnp.maximum(old_peak, top)
            shrink = jnp.exp2((old_peak - new_peak) * EXP_SCALE)
        w = jnp.exp2((s - new_peak) * EXP_SCALE)
        sum_w = jnp.sum(w, axis=0, keepdims=True)
        sum_m = jnp.sum(w * d, axis=0, keepdims=True)
        if not first:
            sum_w = total[stream, j] * shrink + sum_w
            sum_m = moment[stream, j] * shrink + sum_m
        peak[stream, j] = new_peak
        total[stream, j] = sum_w
        moment[stream, j] = sum_m
        save_used(j, new_peak)
        save_w(j, w)
        save_g(j, d)

    def saver(ref, slot):
        def save(j, value):
            ref[slot, j] = value

        return save

    def forward_block(slot, stream, block, visible, first):
        k = kvs[block, :, :HEAD_DIM]
        v = kvs[block, :, HEAD_DIM:]
        for j in range(CHUNKS):
            step_forward(
                stream, k, v, j, visible, first,
                saver(weights, slot), saver(gprobs, slot), saver(used, slot),
            )

    def own_saver(ref):
        def save(j, value):
            ref[j] = value

        return save

    key_row = lax.broadcasted_iota(jnp.int32, (BLOCK, BLOCK), 0)
    own_row = lax.broadcasted_iota(jnp.int32, (HEAD_DIM, BLOCK), 0)
    same = (own_row >> shift) == (jnp.broadcast_to(lane, (HEAD_DIM, BLOCK)) >> shift)
    for j in range(CHUNKS):
        step_forward(
            1, kv_own[:, :HEAD_DIM], kv_own[:, HEAD_DIM:], j, same, True,
            own_saver(weights_own), own_saver(gprobs_own), own_saver(used_own),
        )
    forward_block(15, 0, full_clean, key_row + full_clean * BLOCK < limits(tile_clean, 1), True)
    forward_block(16, 1, full_noisy, key_row + full_noisy * BLOCK < limits(tile_noisy, 0), False)

    def place_of(slot):
        clean = slot < full_clean
        return jnp.where(clean, 0, 1), jnp.where(clean, slot, slot - full_clean)

    def forward_turn(slot, carry):
        stream, block = place_of(slot)
        forward_block(slot, stream, block, None, False)
        return carry

    lax.fori_loop(0, 15, forward_turn, 0)

    for stream in range(2):
        for j in range(CHUNKS):
            inverse = 1.0 / total[stream, j]
            total[stream, j] = inverse
            moment[stream, j] = moment[stream, j] * inverse
            dqt[stream, j] = jnp.zeros((HEAD_DIM, BLOCK), F32)

    def step_backward(stream, kt, j, w, d, seen):
        factor = jnp.exp2((seen - peak[stream, j]) * EXP_SCALE) * total[stream, j]
        p = w * factor
        ds = (p * (d - moment[stream, j])).astype(BF16)
        dv = dot(p.astype(BF16), gh[stream, j])
        dk = dot(ds, qh[stream, j])
        dqt[stream, j] += dot(kt, ds)
        return dk, dv

    def backward_block(slot, stream, block):
        kt = kvs[block, :, :HEAD_DIM].T
        dk = jnp.zeros((BLOCK, HEAD_DIM), F32)
        dv = jnp.zeros((BLOCK, HEAD_DIM), F32)
        for j in range(CHUNKS):
            more_k, more_v = step_backward(
                stream, kt, j, weights[slot, j], gprobs[slot, j], used[slot, j]
            )
            dk += more_k
            dv += more_v
        acc[block, :, :HEAD_DIM] += dk * SCALE
        acc[block, :, HEAD_DIM:] += dv

    kt_own = kv_own[:, :HEAD_DIM].T
    dk = jnp.zeros((HEAD_DIM, HEAD_DIM), F32)
    dv = jnp.zeros((HEAD_DIM, HEAD_DIM), F32)
    for j in range(CHUNKS):
        more_k, more_v = step_backward(1, kt_own, j, weights_own[j], gprobs_own[j], used_own[j])
        dk += more_k
        dv += more_v
    out_own[:, :HEAD_DIM] = (dk * SCALE).astype(BF16)
    out_own[:, HEAD_DIM:] = dv.astype(BF16)

    def backward_turn(slot, carry):
        stream, block = place_of(slot)
        backward_block(slot, stream, block)
        return carry

    lax.fori_loop(0, 15, backward_turn, 0)
    backward_block(15, 0, full_clean)
    backward_block(16, 1, full_noisy)

    for stream, ref in enumerate((dq_clean, dq_noisy)):
        for h in range(2 * CHUNKS):
            at = slice((h % 2) * HEAD_DIM, (h % 2 + 1) * HEAD_DIM)
            tile = dqt[stream, h // 2, :, at]
            ref[:, h * HEAD_DIM : (h + 1) * HEAD_DIM] = (tile.T * SCALE).astype(BF16)
    for part, refs in enumerate(((out_0,), (out_1,), (out_2a, out_2b), (out_3,))):
        place = ((row_y - part) & 3) * blocks_y
        each = blocks_y // len(refs)
        for b in range(blocks_y):
            at = (b % each) * BLOCK
            refs[b // each][at : at + BLOCK, :] = acc[place + b].astype(BF16)


def attention(info, q_clean, g_clean, q_noisy, g_noisy, pieces, kv_own):
    rows, width = q_clean.shape
    span, kv_width = pieces[0].shape
    vmem = pl.BlockSpec(memory_space=pltpu.VMEM)
    shape = jax.ShapeDtypeStruct
    slots = 17
    return pl.pallas_call(
        attention_kernel,
        out_shape=(
            shape((rows, width), BF16),
            shape((rows, width), BF16),
            shape((span, kv_width), BF16),
            shape((span, kv_width), BF16),
            shape((span // 2, kv_width), BF16),
            shape((span // 2, kv_width), BF16),
            shape((span, kv_width), BF16),
            shape((rows, kv_width), BF16),
        ),
        in_specs=[pl.BlockSpec(memory_space=pltpu.SMEM)] + [vmem] * 9,
        out_specs=(vmem,) * 8,
        scratch_shapes=[
            pltpu.VMEM((16, BLOCK, kv_width), BF16),
            pltpu.VMEM((2, CHUNKS, BLOCK, HEAD_DIM), BF16),
            pltpu.VMEM((2, CHUNKS, BLOCK, HEAD_DIM), BF16),
            pltpu.VMEM((2, CHUNKS, HEAD_DIM, BLOCK), BF16),
            pltpu.VMEM((2, CHUNKS, HEAD_DIM, BLOCK), BF16),
            pltpu.VMEM((slots, CHUNKS, BLOCK, BLOCK), F32),
            pltpu.VMEM((slots, CHUNKS, BLOCK, BLOCK), F32),
            pltpu.VMEM((CHUNKS, HEAD_DIM, BLOCK), F32),
            pltpu.VMEM((CHUNKS, HEAD_DIM, BLOCK), F32),
            pltpu.VMEM((2, CHUNKS, 1, BLOCK), F32),
            pltpu.VMEM((2, CHUNKS, 1, BLOCK), F32),
            pltpu.VMEM((2, CHUNKS, 1, BLOCK), F32),
            pltpu.VMEM((slots, CHUNKS, 1, BLOCK), F32),
            pltpu.VMEM((CHUNKS, 1, BLOCK), F32),
            pltpu.VMEM((2, CHUNKS, HEAD_DIM, BLOCK), F32),
            pltpu.VMEM((16, BLOCK, kv_width), F32),
        ],
        compiler_params=pltpu.CompilerParams(vmem_limit_bytes=60 * 1024 * 1024),
    )(info, q_clean, g_clean, q_noisy, g_noisy, *pieces, kv_own)


def in_place_order(pieces, row_y):
    stacked = jnp.stack(pieces)
    ordered = [
        lax.dynamic_index_in_dim(stacked, (row_y - part) & 3, 0, keepdims=False)
        for part in range(4)
    ]
    return jnp.concatenate(ordered, axis=0)


def per_device(tokens, queries, grad_out, w_key, w_value, block_len):
    row_y = lax.axis_index("context_0")
    my_index = lax.axis_index(CONTEXT)
    head = lax.axis_index("head")
    size = lax.axis_size(CONTEXT)
    shard_rows = tokens.shape[2]
    features = tokens.shape[3]
    kv_width = 2 * HEAD_DIM
    weight_pair = jnp.concatenate([w_key, w_value], axis=1)
    noisy_bundle = jnp.concatenate([queries[0, 1], grad_out[0, 1]], axis=1)
    weight_row, noisy_bundle = lax.optimization_barrier(
        (gather_z(weight_pair), turned_over(noisy_bundle, "context_0"))
    )
    noisy_bundle = turned_over(noisy_bundle, "context_1")
    weight_pieces = gather_ring(weight_row, "context_0")
    mine = tokens[0].reshape(2 * shard_rows, features)
    other = swapped(mine)
    width = queries.shape[3]
    full_tokens = jnp.concatenate(
        [jnp.where(head == 0, mine, other), jnp.where(head == 0, other, mine)], axis=1
    )
    weights = in_place_order(weight_pieces, row_y)
    projected, noisy_bundle = lax.optimization_barrier(
        (dot(full_tokens, weights).astype(BF16), noisy_bundle)
    )
    kv_pieces = gather_ring(gather_z(projected[:shard_rows]), "context_0")
    kv_noisy = mirrored(projected[shard_rows:])
    block_size = block_len[0]
    shift = 3 + (block_size > 8).astype(jnp.int32) + (block_size > 16).astype(jnp.int32)
    info = jnp.stack([row_y, my_index, size - 1 - my_index, shift]).astype(jnp.int32)
    dq_clean, dq_noisy, *pair_pieces, pair_noisy = attention(
        info,
        queries[0, 0],
        grad_out[0, 0],
        noisy_bundle[:, :width],
        noisy_bundle[:, width:],
        kv_pieces,
        kv_noisy,
    )
    returned = jnp.concatenate([dq_noisy, pair_noisy], axis=1)
    returned = turned_over(returned, "context_1")
    pair_row, returned = lax.optimization_barrier(
        (reduce_ring(pair_pieces, "context_0").astype(BF16), returned)
    )
    pair_clean, returned = lax.optimization_barrier(
        (scatter_z(pair_row).astype(BF16), turned_over(returned, "context_0"))
    )
    dq_noisy, pair_noisy = returned[:, :width], returned[:, width:]
    pair_grads = jnp.concatenate([pair_clean, pair_noisy], axis=0)

    weight_local = lax.dot_general(
        full_tokens, pair_grads, (((0,), (0,)), ((), ())), preferred_element_type=F32
    ).astype(BF16)
    quarter = weight_local.shape[0] // 4
    half = quarter // 2

    def part_of(step):
        return lax.dynamic_slice_in_dim(weight_local, ((row_y - step) & 3) * quarter, quarter, 0)

    far = part_of(2)
    weight_sum = scatter_z(
        reduce_ring(
            (part_of(0), part_of(1), far[:half], far[half:], part_of(3)), "context_0"
        ).astype(BF16)
    ).astype(BF16)
    copies = jnp.broadcast_to(weight_sum, (lax.axis_size("dp"), *weight_sum.shape))
    weight_sum = jnp.sum(lax.all_to_all(copies, "dp", 0, 0, tiled=True).astype(F32), axis=0)

    terms = lax.dot_general(
        pair_grads, weights, (((1,), (1,)), ((), ())), preferred_element_type=F32
    ).astype(BF16)
    low, high = terms[:, :features], terms[:, features:]
    kept = jnp.where(head == 0, low, high)
    given = swapped(jnp.where(head == 0, high, low))
    grad_x = (kept.astype(F32) + given.astype(F32)).astype(BF16).reshape(tokens.shape)
    grad_query = jnp.stack([dq_clean, dq_noisy])[None]
    return (grad_query, grad_x, weight_sum[:, :HEAD_DIM], weight_sum[:, HEAD_DIM:])


def solution(mesh):
    torus = Mesh(
        mesh.devices.reshape(mesh.shape["dp"], 4, 8, mesh.shape["head"]),
        ("dp", "context_0", "context_1", "head"),
    )
    in_specs = (
        P("dp", None, CONTEXT, "head"),
        P("dp", None, CONTEXT, "head"),
        P("dp", None, CONTEXT, "head"),
        P(CONTEXT, "head"),
        P(CONTEXT, "head"),
        P("dp"),
    )
    out_specs = (
        P("dp", None, CONTEXT, "head"),
        P("dp", None, CONTEXT, "head"),
        P(CONTEXT, "head"),
        P(CONTEXT, "head"),
    )
    return jax.shard_map(
        per_device, mesh=torus, in_specs=in_specs, out_specs=out_specs, check_vma=False
    )
```

```python
import math

import jax
import jax.numpy as jnp
from jax import lax
from jax.experimental import pallas as pl
from jax.experimental.pallas import tpu as pltpu
from jax.sharding import Mesh
from jax.sharding import PartitionSpec as P

HEAD_DIM = 128
CONTEXT = ("context_0", "context_1")
BF16 = jnp.bfloat16
F32 = jnp.float32
MASKED = -1e30
SCALE = 1.0 / math.sqrt(HEAD_DIM)
EXP_SCALE = math.log2(math.e) / math.sqrt(HEAD_DIM)
BLOCK = 256
LANES = 256
CHUNKS = 8 * HEAD_DIM // LANES
PER_CHUNK = LANES // HEAD_DIM


def dot(left, right):
    return jnp.dot(left, right, preferred_element_type=F32)


def shifted(array, axis, step):
    size = lax.axis_size(axis)
    return lax.ppermute(array, axis, [(i, (i + step) % size) for i in range(size)])


def turned_over(array, axis):
    size = lax.axis_size(axis)
    return lax.ppermute(array, axis, [(i, size - 1 - i) for i in range(size)])


def swapped(array):
    return lax.ppermute(array, "head", [(0, 1), (1, 0)])


def gather_z(array):
    copies = jnp.broadcast_to(array, (lax.axis_size("context_1"), *array.shape))
    tiles = lax.all_to_all(copies, "context_1", 0, 0, tiled=True)
    return tiles.reshape(-1, *array.shape[1:])


def gather_ring(array, axis):
    half = array.shape[0] // 2
    before = shifted(array, axis, 1)
    after = shifted(array, axis, -1)
    far_low = shifted(before[:half], axis, 1)
    far_high = shifted(after[half:], axis, -1)
    return array, before, far_low, far_high, after


def reduce_ring(pieces, axis):
    own, before, far_low, far_high, after = pieces
    half = far_low.shape[0]
    got_low = shifted(far_low, axis, 1).astype(F32)
    got_high = shifted(far_high, axis, -1).astype(F32)
    up = after.astype(F32) + jnp.pad(got_low, ((0, half), (0, 0)))
    down = before.astype(F32) + jnp.pad(got_high, ((half, 0), (0, 0)))
    from_before = shifted(up.astype(BF16), axis, 1)
    from_after = shifted(down.astype(BF16), axis, -1)
    return own.astype(F32) + from_before.astype(F32) + from_after.astype(F32)


def scatter_z(array):
    size = lax.axis_size("context_1")
    tiles = array.reshape(size, array.shape[0] // size, array.shape[1])
    tiles = lax.all_to_all(tiles, "context_1", 0, 0, tiled=True)
    return jnp.sum(tiles.astype(F32), axis=0)


def attention_kernel(
    info,
    q_clean,
    g_clean,
    noisy,
    kv_0,
    kv_1,
    kv_2a,
    kv_2b,
    kv_3,
    dq_clean,
    out_noisy,
    out_0,
    out_1,
    out_2a,
    out_2b,
    out_3,
    kvs,
    qh,
    gh,
    qt,
    gt,
    weights,
    gprobs,
    weights_own,
    gprobs_own,
    peak,
    total,
    moment,
    used,
    used_own,
    dqt,
    acc,
):
    row_y = info[0]
    tile_clean = info[1]
    tile_noisy = info[2]
    shift = info[3]
    blocks_y = 4
    full_clean = tile_clean >> 1
    full_noisy = tile_noisy >> 1
    width = q_clean.shape[1]
    for part, sources in enumerate(((kv_0,), (kv_1,), (kv_2a, kv_2b), (kv_3,))):
        place = ((row_y - part) & 3) * blocks_y
        each = blocks_y // len(sources)
        for b in range(blocks_y):
            at = (b % each) * BLOCK
            kvs[place + b] = sources[b // each][at : at + BLOCK, :]
    for stream, (q_ref, g_ref, start) in enumerate(
        ((q_clean, g_clean, 0), (noisy, noisy, width))
    ):
        for h in range(PER_CHUNK * CHUNKS):
            at = slice((h % PER_CHUNK) * HEAD_DIM, (h % PER_CHUNK + 1) * HEAD_DIM)
            for ref, first, rows, turned in ((q_ref, 0, qh, qt), (g_ref, start, gh, gt)):
                first = first + h * HEAD_DIM
                tile = ref[:, first : first + HEAD_DIM]
                rows[stream, h // PER_CHUNK, at, :] = tile
                turned[stream, h // PER_CHUNK, :, at] = tile.T
    acc[...] = jnp.zeros_like(acc)

    lane = lax.broadcasted_iota(jnp.int32, (1, LANES), 1) & (HEAD_DIM - 1)

    def limits(tile, after):
        pos = tile * HEAD_DIM + lane
        return ((pos >> shift) + after) << shift

    def step_forward(stream, k, v, j, visible, first, save_w, save_g, save_used):
        s = dot(k, qt[stream, j])
        d = dot(v, gt[stream, j])
        if visible is not None:
            s = jnp.where(visible, s, MASKED)
        top = jnp.max(s, axis=0, keepdims=True)
        if first:
            new_peak = top
        else:
            old_peak = peak[stream, j]
            new_peak = jnp.maximum(old_peak, top)
            shrink = jnp.exp2((old_peak - new_peak) * EXP_SCALE)
        w = jnp.exp2((s - new_peak) * EXP_SCALE)
        sum_w = jnp.sum(w, axis=0, keepdims=True)
        sum_m = jnp.sum(w * d, axis=0, keepdims=True)
        if not first:
            sum_w = total[stream, j] * shrink + sum_w
            sum_m = moment[stream, j] * shrink + sum_m
        peak[stream, j] = new_peak
        total[stream, j] = sum_w
        moment[stream, j] = sum_m
        save_used(j, new_peak)
        save_w(j, w)
        save_g(j, d)

    def saver(ref, slot):
        def save(j, value):
            ref[slot, j] = value

        return save

    def forward_block(slot, stream, block, visible, first):
        k = kvs[block, :, :HEAD_DIM]
        v = kvs[block, :, HEAD_DIM:]
        for j in range(CHUNKS):
            step_forward(
                stream, k, v, j, visible, first,
                saver(weights, slot), saver(gprobs, slot), saver(used, slot),
            )

    def own_saver(ref):
        def save(j, value):
            ref[j] = value

        return save

    key_row = lax.broadcasted_iota(jnp.int32, (BLOCK, LANES), 0)
    own_row = lax.broadcasted_iota(jnp.int32, (HEAD_DIM, LANES), 0)
    same = (own_row >> shift) == (jnp.broadcast_to(lane, (HEAD_DIM, LANES)) >> shift)
    own_k = noisy[:, 2 * width : 2 * width + HEAD_DIM]
    own_v = noisy[:, 2 * width + HEAD_DIM :]
    for j in range(CHUNKS):
        step_forward(
            1, own_k, own_v, j, same, True,
            own_saver(weights_own), own_saver(gprobs_own), own_saver(used_own),
        )
    forward_block(18, 0, full_clean, key_row + full_clean * BLOCK < limits(tile_clean, 1), True)
    forward_block(19, 1, full_noisy, key_row + full_noisy * BLOCK < limits(tile_noisy, 0), False)

    def place_of(slot):
        clean = slot < full_clean
        return jnp.where(clean, 0, 1), jnp.where(clean, slot, slot - full_clean)

    def forward_turn(slot, carry):
        stream, block = place_of(slot)
        forward_block(slot, stream, block, None, False)
        return carry

    lax.fori_loop(0, full_clean + full_noisy, forward_turn, 0)

    for stream in range(2):
        for j in range(CHUNKS):
            inverse = 1.0 / total[stream, j]
            total[stream, j] = inverse
            moment[stream, j] = moment[stream, j] * inverse
            dqt[stream, j] = jnp.zeros((HEAD_DIM, LANES), F32)

    def step_backward(stream, kt, j, w, d, seen):
        factor = jnp.exp2((seen - peak[stream, j]) * EXP_SCALE) * total[stream, j]
        p = w * factor
        ds = (p * (d - moment[stream, j])).astype(BF16)
        dv = dot(p.astype(BF16), gh[stream, j])
        dk = dot(ds, qh[stream, j])
        dqt[stream, j] += dot(kt, ds)
        return dk, dv

    def backward_block(slot, stream, block):
        kt = kvs[block, :, :HEAD_DIM].T
        dk = jnp.zeros((BLOCK, HEAD_DIM), F32)
        dv = jnp.zeros((BLOCK, HEAD_DIM), F32)
        for j in range(CHUNKS):
            more_k, more_v = step_backward(
                stream, kt, j, weights[slot, j], gprobs[slot, j], used[slot, j]
            )
            dk += more_k
            dv += more_v
        acc[block, :, :HEAD_DIM] += dk * SCALE
        acc[block, :, HEAD_DIM:] += dv

    kt_own = own_k.T
    dk = jnp.zeros((HEAD_DIM, HEAD_DIM), F32)
    dv = jnp.zeros((HEAD_DIM, HEAD_DIM), F32)
    for j in range(CHUNKS):
        more_k, more_v = step_backward(1, kt_own, j, weights_own[j], gprobs_own[j], used_own[j])
        dk += more_k
        dv += more_v
    out_noisy[:, width : width + HEAD_DIM] = (dk * SCALE).astype(BF16)
    out_noisy[:, width + HEAD_DIM :] = dv.astype(BF16)

    def backward_turn(slot, carry):
        stream, block = place_of(slot)
        backward_block(slot, stream, block)
        return carry

    lax.fori_loop(0, full_clean + full_noisy, backward_turn, 0)
    backward_block(18, 0, full_clean)
    backward_block(19, 1, full_noisy)

    for stream, ref in enumerate((dq_clean, out_noisy)):
        for h in range(PER_CHUNK * CHUNKS):
            at = slice((h % PER_CHUNK) * HEAD_DIM, (h % PER_CHUNK + 1) * HEAD_DIM)
            tile = dqt[stream, h // PER_CHUNK, :, at]
            ref[:, h * HEAD_DIM : (h + 1) * HEAD_DIM] = (tile.T * SCALE).astype(BF16)
    for part, refs in enumerate(((out_0,), (out_1,), (out_2a, out_2b), (out_3,))):
        place = ((row_y - part) & 3) * blocks_y
        each = blocks_y // len(refs)
        for b in range(blocks_y):
            at = (b % each) * BLOCK
            refs[b // each][at : at + BLOCK, :] = acc[place + b].astype(BF16)


def attention(info, q_clean, g_clean, noisy, pieces):
    rows, width = q_clean.shape
    span, kv_width = pieces[0].shape
    vmem = pl.BlockSpec(memory_space=pltpu.VMEM)
    shape = jax.ShapeDtypeStruct
    slots = 20
    return pl.pallas_call(
        attention_kernel,
        out_shape=(
            shape((rows, width), BF16),
            shape((rows, width + kv_width), BF16),
            shape((span, kv_width), BF16),
            shape((span, kv_width), BF16),
            shape((span // 2, kv_width), BF16),
            shape((span // 2, kv_width), BF16),
            shape((span, kv_width), BF16),
        ),
        in_specs=[pl.BlockSpec(memory_space=pltpu.SMEM)] + [vmem] * 8,
        out_specs=(vmem,) * 7,
        scratch_shapes=[
            pltpu.VMEM((16, BLOCK, kv_width), BF16),
            pltpu.VMEM((2, CHUNKS, LANES, HEAD_DIM), BF16),
            pltpu.VMEM((2, CHUNKS, LANES, HEAD_DIM), BF16),
            pltpu.VMEM((2, CHUNKS, HEAD_DIM, LANES), BF16),
            pltpu.VMEM((2, CHUNKS, HEAD_DIM, LANES), BF16),
            pltpu.VMEM((slots, CHUNKS, BLOCK, LANES), F32),
            pltpu.VMEM((slots, CHUNKS, BLOCK, LANES), F32),
            pltpu.VMEM((CHUNKS, HEAD_DIM, LANES), F32),
            pltpu.VMEM((CHUNKS, HEAD_DIM, LANES), F32),
            pltpu.VMEM((2, CHUNKS, 1, LANES), F32),
            pltpu.VMEM((2, CHUNKS, 1, LANES), F32),
            pltpu.VMEM((2, CHUNKS, 1, LANES), F32),
            pltpu.VMEM((slots, CHUNKS, 1, LANES), F32),
            pltpu.VMEM((CHUNKS, 1, LANES), F32),
            pltpu.VMEM((2, CHUNKS, HEAD_DIM, LANES), F32),
            pltpu.VMEM((16, BLOCK, kv_width), F32),
        ],
        cost_estimate=pl.CostEstimate(
            flops=6 * 10**9, transcendentals=9 * 10**6, bytes_accessed=8 * 10**6
        ),
        compiler_params=pltpu.CompilerParams(vmem_limit_bytes=60 * 1024 * 1024),
    )(info, q_clean, g_clean, noisy, *pieces)


def columns_over_rows(mine, row_y):
    part = mine.shape[1] // 4
    received = []
    for k in range(4):
        pairs = [
            (2 * y + h, 2 * (2 * h + ((y ^ k) >> 1)) + ((y ^ k) & 1)) for y in range(4) for h in range(2)
        ]
        sent = lax.dynamic_slice_in_dim(mine, (row_y ^ k) * part, part, 1)
        received.append(lax.ppermute(sent, ("context_0", "head"), pairs))
    return received


def per_device(tokens, queries, grad_out, w_key, w_value, block_len):
    row_y = lax.axis_index("context_0")
    my_index = lax.axis_index(CONTEXT)
    head = lax.axis_index("head")
    shard_rows = tokens.shape[2]
    features = tokens.shape[3]
    width = queries.shape[3]
    rows = 2 * shard_rows
    over_rows = (((0,), (0,)), ((), ()))
    over_columns = (((1,), (1,)), ((), ()))
    weight_row = gather_z(jnp.concatenate([w_key, w_value], axis=1))
    received = columns_over_rows(tokens[0].reshape(rows, features), row_y)
    received[3], weight_row = lax.optimization_barrier((received[3], weight_row))
    here = jnp.concatenate(received, axis=0)
    there = jnp.concatenate([swapped(received[k ^ 1]) for k in range(4)], axis=0)
    base = 2 * (row_y & 1) + head
    half = weight_row.shape[0] // 2
    partial = dot(here, lax.dynamic_slice_in_dim(weight_row, head * half, half, 0)) + dot(
        there, lax.dynamic_slice_in_dim(weight_row, (1 - head) * half, half, 0)
    )

    def partial_for(step):
        return lax.dynamic_slice_in_dim(partial, (base ^ ((row_y + step) & 3)) * rows, rows, 0)

    whole = partial_for(0)
    for s in range(1, 4):
        whole = whole + shifted(partial_for(s).astype(BF16), "context_0", s).astype(F32)
    projected = whole.astype(BF16)

    noisy = jnp.concatenate([queries[0, 1], grad_out[0, 1], projected[shard_rows:]], axis=1)
    kv_row, noisy = lax.optimization_barrier(
        (gather_z(projected[:shard_rows]), turned_over(noisy, "context_0"))
    )
    kv_pieces = gather_ring(kv_row, "context_0")
    kv_pieces, noisy, weight_row = lax.optimization_barrier((kv_pieces, noisy, weight_row))
    weight_near = (shifted(weight_row, "context_0", 1), shifted(weight_row, "context_0", -1))

    block_size = block_len[0]
    shift = 3 + (block_size > 8).astype(jnp.int32) + (block_size > 16).astype(jnp.int32)
    rows_z = lax.axis_size("context_1")
    noisy_index = (3 - row_y) * rows_z + lax.axis_index("context_1")
    info = jnp.stack([row_y, my_index, noisy_index, shift]).astype(jnp.int32)
    dq_clean, returned, *pair_pieces = attention(
        info, queries[0, 0], grad_out[0, 0], noisy, kv_pieces
    )
    pair_pieces, returned, weight_near = lax.optimization_barrier(
        (pair_pieces, returned, weight_near)
    )
    pair_row, returned, weight_near = lax.optimization_barrier(
        (reduce_ring(pair_pieces, "context_0").astype(BF16), returned, weight_near)
    )
    before, after = weight_near
    weight_far = (shifted(before[:half], "context_0", 1), shifted(after[half:], "context_0", -1))
    pair_clean, returned, weight_far = lax.optimization_barrier(
        (scatter_z(pair_row).astype(BF16), turned_over(returned, "context_0"), weight_far)
    )
    dq_noisy, pair_noisy = returned[:, :width], returned[:, width:]
    pair_grads = jnp.concatenate([pair_clean, pair_noisy], axis=0)

    around = jnp.zeros((4 * rows, pair_grads.shape[1]), BF16)
    for s in range(4):
        piece = shifted(pair_grads, "context_0", s) if s else pair_grads
        around = lax.dynamic_update_slice_in_dim(
            around, piece, (base ^ ((row_y - s) & 3)) * rows, 0
        )
    local_here = lax.dot_general(here, around, over_rows, preferred_element_type=F32)
    local_there = lax.dot_general(there, around, over_rows, preferred_element_type=F32)
    weight_local = jnp.stack(
        [
            jnp.where(head == 0, local_here, local_there).astype(BF16),
            jnp.where(head == 0, local_there, local_here).astype(BF16),
        ]
    ).reshape(2 * half, -1)
    weight_local, pair_grads = lax.optimization_barrier((weight_local, pair_grads))
    other_pair, weight_row, before, after, weight_far = lax.optimization_barrier(
        (swapped(pair_grads), weight_row, before, after, weight_far)
    )
    weight_sum = scatter_z(weight_local).astype(BF16)
    copies = jnp.broadcast_to(weight_sum, (lax.axis_size("dp"), *weight_sum.shape))
    weight_sum = jnp.sum(lax.all_to_all(copies, "dp", 0, 0, tiled=True).astype(F32), axis=0)

    stacked = jnp.stack([weight_row, before, jnp.concatenate(weight_far, axis=0), after])

    def weight_half(which):
        return jnp.concatenate(
            [
                lax.dynamic_index_in_dim(stacked, (row_y - 2 * which - i) & 3, 0, keepdims=False)
                for i in range(2)
            ],
            axis=0,
        )

    kept = weight_half(head)
    given = swapped(weight_half(1 - head))
    grad_x = lax.dot_general(pair_grads, kept, over_columns, preferred_element_type=F32)
    grad_x = grad_x + lax.dot_general(
        other_pair, given, over_columns, preferred_element_type=F32
    )
    grad_x = grad_x.astype(BF16).reshape(tokens.shape)
    grad_query = jnp.stack([dq_clean, dq_noisy])[None]
    return (grad_query, grad_x, weight_sum[:, :HEAD_DIM], weight_sum[:, HEAD_DIM:])


def solution(mesh):
    torus = Mesh(
        mesh.devices.reshape(mesh.shape["dp"], 4, 8, mesh.shape["head"]),
        ("dp", "context_0", "context_1", "head"),
    )
    in_specs = (
        P("dp", None, CONTEXT, "head"),
        P("dp", None, CONTEXT, "head"),
        P("dp", None, CONTEXT, "head"),
        P(CONTEXT, "head"),
        P(CONTEXT, "head"),
        P("dp"),
    )
    out_specs = (
        P("dp", None, CONTEXT, "head"),
        P("dp", None, CONTEXT, "head"),
        P(CONTEXT, "head"),
        P(CONTEXT, "head"),
    )
    return jax.shard_map(
        per_device, mesh=torus, in_specs=in_specs, out_specs=out_specs, check_vma=False
    )
```

```python
import math

import jax
import jax.numpy as jnp
from jax import lax
from jax.experimental import pallas as pl
from jax.experimental.pallas import tpu as pltpu
from jax.sharding import Mesh
from jax.sharding import PartitionSpec as P

HEAD_DIM = 128
CONTEXT = ("context_0", "context_1")
BF16 = jnp.bfloat16
F32 = jnp.float32
MASKED = -1e30
SCALE = 1.0 / math.sqrt(HEAD_DIM)
EXP_SCALE = math.log2(math.e) / math.sqrt(HEAD_DIM)
BLOCK = 256
LANES = 256
CHUNKS = 8 * HEAD_DIM // LANES
PER_CHUNK = LANES // HEAD_DIM


def dot(left, right):
    return jnp.dot(left, right, preferred_element_type=F32)


def shifted(array, axis, step):
    size = lax.axis_size(axis)
    return lax.ppermute(array, axis, [(i, (i + step) % size) for i in range(size)])


def turned_over(array, axis):
    size = lax.axis_size(axis)
    return lax.ppermute(array, axis, [(i, size - 1 - i) for i in range(size)])


def swapped(array):
    return lax.ppermute(array, "head", [(0, 1), (1, 0)])


def gather_z(array):
    copies = jnp.broadcast_to(array, (lax.axis_size("context_1"), *array.shape))
    tiles = lax.all_to_all(copies, "context_1", 0, 0, tiled=True)
    return tiles.reshape(-1, *array.shape[1:])


def gather_ring(array, axis):
    half = array.shape[0] // 2
    before = shifted(array, axis, 1)
    after = shifted(array, axis, -1)
    far_low = shifted(before[:half], axis, 1)
    far_high = shifted(after[half:], axis, -1)
    return array, before, far_low, far_high, after


def reduce_ring(pieces, axis):
    own, before, far_low, far_high, after = pieces
    half = far_low.shape[0]
    got_low = shifted(far_low, axis, 1).astype(F32)
    got_high = shifted(far_high, axis, -1).astype(F32)
    up = after.astype(F32) + jnp.pad(got_low, ((0, half), (0, 0)))
    down = before.astype(F32) + jnp.pad(got_high, ((half, 0), (0, 0)))
    from_before = shifted(up.astype(BF16), axis, 1)
    from_after = shifted(down.astype(BF16), axis, -1)
    return own.astype(F32) + from_before.astype(F32) + from_after.astype(F32)


def scatter_z(array):
    size = lax.axis_size("context_1")
    tiles = array.reshape(size, array.shape[0] // size, array.shape[1])
    tiles = lax.all_to_all(tiles, "context_1", 0, 0, tiled=True)
    return jnp.sum(tiles.astype(F32), axis=0)


def attention_kernel(
    info,
    q_clean,
    g_clean,
    noisy,
    kv_0,
    kv_1,
    kv_2a,
    kv_2b,
    kv_3,
    dq_clean,
    out_noisy,
    out_0,
    out_1,
    out_2a,
    out_2b,
    out_3,
    kvs,
    qh,
    gh,
    qt,
    gt,
    weights,
    gprobs,
    weights_own,
    gprobs_own,
    peak,
    total,
    moment,
    used,
    used_own,
    dqt,
    acc,
):
    row_y = info[0]
    tile_clean = info[1]
    tile_noisy = info[2]
    shift = info[3]
    blocks_y = 4
    full_clean = tile_clean >> 1
    full_noisy = tile_noisy >> 1
    width = q_clean.shape[1]
    for part, sources in enumerate(((kv_0,), (kv_1,), (kv_2a, kv_2b), (kv_3,))):
        place = ((row_y - part) & 3) * blocks_y
        each = blocks_y // len(sources)
        for b in range(blocks_y):
            at = (b % each) * BLOCK
            kvs[place + b] = sources[b // each][at : at + BLOCK, :]
    for stream, (q_ref, g_ref, start) in enumerate(
        ((q_clean, g_clean, 0), (noisy, noisy, width))
    ):
        for h in range(PER_CHUNK * CHUNKS):
            at = slice((h % PER_CHUNK) * HEAD_DIM, (h % PER_CHUNK + 1) * HEAD_DIM)
            for ref, first, rows, turned in ((q_ref, 0, qh, qt), (g_ref, start, gh, gt)):
                first = first + h * HEAD_DIM
                tile = ref[:, first : first + HEAD_DIM]
                rows[stream, h // PER_CHUNK, at, :] = tile
                turned[stream, h // PER_CHUNK, :, at] = tile.T
    acc[...] = jnp.zeros_like(acc)

    lane = lax.broadcasted_iota(jnp.int32, (1, LANES), 1) & (HEAD_DIM - 1)

    def limits(tile, after):
        pos = tile * HEAD_DIM + lane
        return ((pos >> shift) + after) << shift

    def step_forward(stream, k, v, j, visible, first, save_w, save_g, save_used):
        s = dot(k, qt[stream, j])
        d = dot(v, gt[stream, j])
        if visible is not None:
            s = jnp.where(visible, s, MASKED)
        top = jnp.max(s, axis=0, keepdims=True)
        if first:
            new_peak = top
        else:
            old_peak = peak[stream, j]
            new_peak = jnp.maximum(old_peak, top)
            shrink = jnp.exp2((old_peak - new_peak) * EXP_SCALE)
        w = jnp.exp2((s - new_peak) * EXP_SCALE)
        sum_w = jnp.sum(w, axis=0, keepdims=True)
        sum_m = jnp.sum(w * d, axis=0, keepdims=True)
        if not first:
            sum_w = total[stream, j] * shrink + sum_w
            sum_m = moment[stream, j] * shrink + sum_m
        peak[stream, j] = new_peak
        total[stream, j] = sum_w
        moment[stream, j] = sum_m
        save_used(j, new_peak)
        save_w(j, w)
        save_g(j, d)

    def saver(ref, slot):
        def save(j, value):
            ref[slot, j] = value

        return save

    def forward_block(slot, stream, block, visible, first):
        k = kvs[block, :, :HEAD_DIM]
        v = kvs[block, :, HEAD_DIM:]
        for j in range(CHUNKS):
            step_forward(
                stream, k, v, j, visible, first,
                saver(weights, slot), saver(gprobs, slot), saver(used, slot),
            )

    def own_saver(ref):
        def save(j, value):
            ref[j] = value

        return save

    key_row = lax.broadcasted_iota(jnp.int32, (BLOCK, LANES), 0)
    own_row = lax.broadcasted_iota(jnp.int32, (HEAD_DIM, LANES), 0)
    same = (own_row >> shift) == (jnp.broadcast_to(lane, (HEAD_DIM, LANES)) >> shift)
    own_k = noisy[:, 2 * width : 2 * width + HEAD_DIM]
    own_v = noisy[:, 2 * width + HEAD_DIM :]
    for j in range(CHUNKS):
        step_forward(
            1, own_k, own_v, j, same, True,
            own_saver(weights_own), own_saver(gprobs_own), own_saver(used_own),
        )
    forward_block(18, 0, full_clean, key_row + full_clean * BLOCK < limits(tile_clean, 1), True)
    forward_block(19, 1, full_noisy, key_row + full_noisy * BLOCK < limits(tile_noisy, 0), False)

    def place_of(slot):
        clean = slot < full_clean
        return jnp.where(clean, 0, 1), jnp.where(clean, slot, slot - full_clean)

    def forward_turn(slot, carry):
        stream, block = place_of(slot)
        forward_block(slot, stream, block, None, False)
        return carry

    lax.fori_loop(0, full_clean + full_noisy, forward_turn, 0)

    for stream in range(2):
        for j in range(CHUNKS):
            inverse = 1.0 / total[stream, j]
            total[stream, j] = inverse
            moment[stream, j] = moment[stream, j] * inverse
            dqt[stream, j] = jnp.zeros((HEAD_DIM, LANES), F32)

    def step_backward(stream, kt, j, w, d, seen):
        factor = jnp.exp2((seen - peak[stream, j]) * EXP_SCALE) * total[stream, j]
        p = w * factor
        ds = (p * (d - moment[stream, j])).astype(BF16)
        dv = dot(p.astype(BF16), gh[stream, j])
        dk = dot(ds, qh[stream, j])
        dqt[stream, j] += dot(kt, ds)
        return dk, dv

    def backward_block(slot, stream, block):
        kt = kvs[block, :, :HEAD_DIM].T
        dk = jnp.zeros((BLOCK, HEAD_DIM), F32)
        dv = jnp.zeros((BLOCK, HEAD_DIM), F32)
        for j in range(CHUNKS):
            more_k, more_v = step_backward(
                stream, kt, j, weights[slot, j], gprobs[slot, j], used[slot, j]
            )
            dk += more_k
            dv += more_v
        acc[block, :, :HEAD_DIM] += dk * SCALE
        acc[block, :, HEAD_DIM:] += dv

    kt_own = own_k.T
    dk = jnp.zeros((HEAD_DIM, HEAD_DIM), F32)
    dv = jnp.zeros((HEAD_DIM, HEAD_DIM), F32)
    for j in range(CHUNKS):
        more_k, more_v = step_backward(1, kt_own, j, weights_own[j], gprobs_own[j], used_own[j])
        dk += more_k
        dv += more_v
    out_noisy[:, width : width + HEAD_DIM] = (dk * SCALE).astype(BF16)
    out_noisy[:, width + HEAD_DIM :] = dv.astype(BF16)

    def backward_turn(slot, carry):
        stream, block = place_of(slot)
        backward_block(slot, stream, block)
        return carry

    lax.fori_loop(0, full_clean + full_noisy, backward_turn, 0)
    backward_block(18, 0, full_clean)
    backward_block(19, 1, full_noisy)

    for stream, ref in enumerate((dq_clean, out_noisy)):
        for h in range(PER_CHUNK * CHUNKS):
            at = slice((h % PER_CHUNK) * HEAD_DIM, (h % PER_CHUNK + 1) * HEAD_DIM)
            tile = dqt[stream, h // PER_CHUNK, :, at]
            ref[:, h * HEAD_DIM : (h + 1) * HEAD_DIM] = (tile.T * SCALE).astype(BF16)
    for part, refs in enumerate(((out_0,), (out_1,), (out_2a, out_2b), (out_3,))):
        place = ((row_y - part) & 3) * blocks_y
        each = blocks_y // len(refs)
        for b in range(blocks_y):
            at = (b % each) * BLOCK
            refs[b // each][at : at + BLOCK, :] = acc[place + b].astype(BF16)


def attention(info, q_clean, g_clean, noisy, pieces):
    rows, width = q_clean.shape
    span, kv_width = pieces[0].shape
    vmem = pl.BlockSpec(memory_space=pltpu.VMEM)
    shape = jax.ShapeDtypeStruct
    slots = 20
    return pl.pallas_call(
        attention_kernel,
        out_shape=(
            shape((rows, width), BF16),
            shape((rows, width + kv_width), BF16),
            shape((span, kv_width), BF16),
            shape((span, kv_width), BF16),
            shape((span // 2, kv_width), BF16),
            shape((span // 2, kv_width), BF16),
            shape((span, kv_width), BF16),
        ),
        in_specs=[pl.BlockSpec(memory_space=pltpu.SMEM)] + [vmem] * 8,
        out_specs=(vmem,) * 7,
        scratch_shapes=[
            pltpu.VMEM((16, BLOCK, kv_width), BF16),
            pltpu.VMEM((2, CHUNKS, LANES, HEAD_DIM), BF16),
            pltpu.VMEM((2, CHUNKS, LANES, HEAD_DIM), BF16),
            pltpu.VMEM((2, CHUNKS, HEAD_DIM, LANES), BF16),
            pltpu.VMEM((2, CHUNKS, HEAD_DIM, LANES), BF16),
            pltpu.VMEM((slots, CHUNKS, BLOCK, LANES), F32),
            pltpu.VMEM((slots, CHUNKS, BLOCK, LANES), F32),
            pltpu.VMEM((CHUNKS, HEAD_DIM, LANES), F32),
            pltpu.VMEM((CHUNKS, HEAD_DIM, LANES), F32),
            pltpu.VMEM((2, CHUNKS, 1, LANES), F32),
            pltpu.VMEM((2, CHUNKS, 1, LANES), F32),
            pltpu.VMEM((2, CHUNKS, 1, LANES), F32),
            pltpu.VMEM((slots, CHUNKS, 1, LANES), F32),
            pltpu.VMEM((CHUNKS, 1, LANES), F32),
            pltpu.VMEM((2, CHUNKS, HEAD_DIM, LANES), F32),
            pltpu.VMEM((16, BLOCK, kv_width), F32),
        ],
        cost_estimate=pl.CostEstimate(
            flops=6 * 10**9, transcendentals=9 * 10**6, bytes_accessed=8 * 10**6
        ),
        compiler_params=pltpu.CompilerParams(vmem_limit_bytes=60 * 1024 * 1024),
    )(info, q_clean, g_clean, noisy, *pieces)


def halves_kernel(info, own, before, far_low, far_high, after, kept, given):
    row_y = info[0]
    head = info[1]
    span = own.shape[0]
    half = span // 2
    for part, sources in enumerate(((own,), (before,), (far_low, far_high), (after,))):
        block = (row_y - part) & 3
        place = block & 1
        for target, wanted in ((kept, head), (given, 1 - head)):

            @pl.when((block >> 1) == wanted)
            def _():
                for i, source in enumerate(sources):
                    target[place, i * half : i * half + source.shape[0], :] = source[...]


def weight_halves(row_y, head, own, before, far_low, far_high, after):
    vmem = pl.BlockSpec(memory_space=pltpu.VMEM)
    shape = jax.ShapeDtypeStruct((2, *own.shape), BF16)
    return pl.pallas_call(
        halves_kernel,
        out_shape=(shape, shape),
        in_specs=[pl.BlockSpec(memory_space=pltpu.SMEM)] + [vmem] * 5,
        out_specs=(vmem, vmem),
    )(jnp.stack([row_y, head]).astype(jnp.int32), own, before, far_low, far_high, after)


def columns_over_rows(mine, row_y):
    part = mine.shape[1] // 4
    received = []
    for k in range(4):
        pairs = [
            (2 * y + h, 2 * (2 * h + ((y ^ k) >> 1)) + ((y ^ k) & 1)) for y in range(4) for h in range(2)
        ]
        sent = lax.dynamic_slice_in_dim(mine, (row_y ^ k) * part, part, 1)
        received.append(lax.ppermute(sent, ("context_0", "head"), pairs))
    return received


def per_device(tokens, queries, grad_out, w_key, w_value, block_len):
    row_y = lax.axis_index("context_0")
    my_index = lax.axis_index(CONTEXT)
    head = lax.axis_index("head")
    shard_rows = tokens.shape[2]
    features = tokens.shape[3]
    width = queries.shape[3]
    rows = 2 * shard_rows
    kv_width = 2 * HEAD_DIM
    over_rows = (((0,), (0,)), ((), ()))
    over_columns = (((1,), (1,)), ((), ()))
    weight_row = gather_z(jnp.concatenate([w_key, w_value], axis=1))
    received = columns_over_rows(tokens[0].reshape(rows, features), row_y)
    received[3], weight_row = lax.optimization_barrier((received[3], weight_row))
    here = jnp.concatenate(received, axis=0)
    there = jnp.concatenate([swapped(received[k ^ 1]) for k in range(4)], axis=0)
    base = 2 * (row_y & 1) + head
    half = weight_row.shape[0] // 2
    partial = dot(here, lax.dynamic_slice_in_dim(weight_row, head * half, half, 0)) + dot(
        there, lax.dynamic_slice_in_dim(weight_row, (1 - head) * half, half, 0)
    )

    def partial_for(step):
        return lax.dynamic_slice_in_dim(partial, (base ^ ((row_y + step) & 3)) * rows, rows, 0)

    whole = partial_for(0)
    for s in range(1, 4):
        whole = whole + shifted(partial_for(s).astype(BF16), "context_0", s).astype(F32)
    projected = whole.astype(BF16)

    noisy = jnp.concatenate([queries[0, 1], grad_out[0, 1], projected[shard_rows:]], axis=1)
    kv_row, noisy = lax.optimization_barrier(
        (gather_z(projected[:shard_rows]), turned_over(noisy, "context_0"))
    )
    kv_pieces = gather_ring(kv_row, "context_0")
    kv_pieces, noisy, weight_row = lax.optimization_barrier((kv_pieces, noisy, weight_row))
    weight_near = (shifted(weight_row, "context_0", 1), shifted(weight_row, "context_0", -1))

    block_size = block_len[0]
    shift = 3 + (block_size > 8).astype(jnp.int32) + (block_size > 16).astype(jnp.int32)
    rows_z = lax.axis_size("context_1")
    noisy_index = (3 - row_y) * rows_z + lax.axis_index("context_1")
    info = jnp.stack([row_y, my_index, noisy_index, shift]).astype(jnp.int32)
    dq_clean, returned, *pair_pieces = attention(
        info, queries[0, 0], grad_out[0, 0], noisy, kv_pieces
    )
    pair_pieces, returned, weight_near = lax.optimization_barrier(
        (pair_pieces, returned, weight_near)
    )
    pair_row, returned, weight_near = lax.optimization_barrier(
        (reduce_ring(pair_pieces, "context_0").astype(BF16), returned, weight_near)
    )
    before, after = weight_near
    weight_far = (shifted(before[:half], "context_0", 1), shifted(after[half:], "context_0", -1))
    pair_clean, returned, weight_far = lax.optimization_barrier(
        (scatter_z(pair_row).astype(BF16), turned_over(returned, "context_0"), weight_far)
    )
    dq_noisy, pair_noisy = returned[:, :width], returned[:, width:]
    pair_grads = jnp.concatenate([pair_clean, pair_noisy], axis=0)

    around = jnp.zeros((4 * rows, pair_grads.shape[1]), BF16)
    for s in range(4):
        piece = shifted(pair_grads, "context_0", s) if s else pair_grads
        around = lax.dynamic_update_slice_in_dim(
            around, piece, (base ^ ((row_y - s) & 3)) * rows, 0
        )
    kept, given = weight_halves(row_y, head, weight_row, before, *weight_far, after)
    around, kept, given = lax.optimization_barrier((around, kept, given))
    local_here = lax.dot_general(here, around, over_rows, preferred_element_type=F32)
    local_there = lax.dot_general(there, around, over_rows, preferred_element_type=F32)
    weight_local = jnp.stack(
        [
            jnp.where(head == 0, local_here, local_there).astype(BF16),
            jnp.where(head == 0, local_there, local_here).astype(BF16),
        ]
    ).reshape(2 * half, -1)
    weight_local, pair_grads = lax.optimization_barrier((weight_local, pair_grads))
    other_pair = swapped(pair_grads)
    given = swapped(given)
    weight_sum, given = lax.optimization_barrier((scatter_z(weight_local).astype(BF16), given))
    kept = kept.reshape(features, kv_width)
    given = given.reshape(features, kv_width)
    copies = jnp.broadcast_to(weight_sum, (lax.axis_size("dp"), *weight_sum.shape))
    weight_tiles = lax.all_to_all(copies, "dp", 0, 0, tiled=True)
    weight_sums = [
        jnp.sum(weight_tiles[..., at : at + HEAD_DIM].astype(F32), axis=0) for at in (0, HEAD_DIM)
    ]
    grad_x = lax.dot_general(pair_grads, kept, over_columns, preferred_element_type=F32)
    grad_x = grad_x + lax.dot_general(
        other_pair, given, over_columns, preferred_element_type=F32
    )
    grad_x = grad_x.astype(BF16).reshape(tokens.shape)
    grad_query = jnp.stack([dq_clean, dq_noisy])[None]
    return (grad_query, grad_x, *weight_sums)


def solution(mesh):
    torus = Mesh(
        mesh.devices.reshape(mesh.shape["dp"], 4, 8, mesh.shape["head"]),
        ("dp", "context_0", "context_1", "head"),
    )
    in_specs = (
        P("dp", None, CONTEXT, "head"),
        P("dp", None, CONTEXT, "head"),
        P("dp", None, CONTEXT, "head"),
        P(CONTEXT, "head"),
        P(CONTEXT, "head"),
        P("dp"),
    )
    out_specs = (
        P("dp", None, CONTEXT, "head"),
        P("dp", None, CONTEXT, "head"),
        P(CONTEXT, "head"),
        P(CONTEXT, "head"),
    )
    return jax.shard_map(
        per_device, mesh=torus, in_specs=in_specs, out_specs=out_specs, check_vma=False
    )
```
